32 devices in a mesh: blk: 4 (over x, core), heads: 8 (over z, y).
Axes of the slice: x: 2, y: 2, z: 4, core: 2. Of those that a mesh axis runs over, the one named last changes fastest.
Arguments:
- queries: bfloat16 [2048, 8192], P('blk', 'heads'), may hold values from -6 to 6
- key_rows: bfloat16 [2048, 1024], P('blk'), may hold values from -6 to 6
- value_head_rows: bfloat16 [2048, 1024], P('blk'), may hold values from -6 to 6
- out_weight: bfloat16 [8192, 4096], P('heads', 'blk'), may hold values from -0.0625 to 0.0625
Outputs:
- projected: bfloat16 [2048, 4096], P(('blk', 'heads'))
The draws below stay inside these ranges and needn't reach their ends.
All inputs are finite; a program needn't handle non-finite values.
Results may differ from the reference program's by a relative error of at most 0.013.
Values may be sent and summed in bfloat16 or wider, within the bound.
A program may use at most 64 MiB of HBM per device.

```python
import jax
import jax.numpy as jnp
from jax import lax

QUERY_HEADS = 64
KEY_VALUE_HEADS = 8
HEAD_SIZE = 128
DOUT = 4096
SEQUENCE_TOKENS = 2048
HPD = 8
N_HEADS = 8


def draw_queries(key, part):
    random_subkey = jax.random.fold_in(key, 11)
    value_entries = jnp.clip(jax.random.normal(random_subkey, (SEQUENCE_TOKENS, QUERY_HEADS * HEAD_SIZE), jnp.float32) * 1.41, -6.0, 6.0)
    return value_entries.astype(jnp.bfloat16)


def draw_key_rows(key, part):
    random_subkey = jax.random.fold_in(key, 12)
    value_entries = jnp.clip(jax.random.normal(random_subkey, (SEQUENCE_TOKENS, KEY_VALUE_HEADS * HEAD_SIZE), jnp.float32) * 1.41, -6.0, 6.0)
    return value_entries.astype(jnp.bfloat16)


def level_of(rng, dims, shards, smallest, top_value):
    loudness, own = 1.0, jax.random.fold_in(rng, 6)
    for position, blocks in shards:
        heights = jnp.exp(jax.random.uniform(jax.random.fold_in(own, position), (blocks,), jnp.float32, smallest / len(shards), top_value / len(shards)))
        loudness = loudness * jnp.repeat(heights, dims[position] // blocks).reshape([-1 if axis == position else 1 for axis in range(len(dims))])
    return loudness


def noise(stream_key, dims, width, most, cuts=(), held_as=jnp.bfloat16):
    values = jax.random.normal(stream_key, dims, jnp.float32) * width
    if len(cuts) > 0:
        values = level_of(stream_key, dims, cuts, -0.22, 0.18) * values
    return jnp.clip(values, min=-most, max=most).astype(held_as)


def setup_inputs(seed: int = 0) -> dict:
    key_list = jax.random.split(jax.random.key(seed), 5)
    return {
        "queries": draw_queries(jax.random.fold_in(key_list[4], 71), 0),
        "key_rows": draw_key_rows(jax.random.fold_in(key_list[4], 71), 0),
        "value_head_rows": noise(key_list[2], (SEQUENCE_TOKENS, KEY_VALUE_HEADS * HEAD_SIZE), 1.0, 6.0, ((0, 4),)),
        "out_weight": noise(key_list[3], (QUERY_HEADS * HEAD_SIZE, DOUT), (QUERY_HEADS * HEAD_SIZE) ** -0.5, 0.0625, ((0, 8), (1, 4))),
    }


def reference(queries, key_rows, value_head_rows, out_weight):
    group_width = QUERY_HEADS // KEY_VALUE_HEADS
    inv_root = HEAD_SIZE ** -0.5
    positions = jnp.arange(SEQUENCE_TOKENS, dtype=jnp.int32)
    visible = positions[:, None] >= positions[None, :]

    def one_head(head_number):
        query_cols = lax.dynamic_slice_in_dim(queries, head_number * HEAD_SIZE, HEAD_SIZE, 1)
        shared = (head_number // group_width) * HEAD_SIZE
        key_cols = lax.dynamic_slice_in_dim(key_rows, shared, HEAD_SIZE, 1)
        value_cols = lax.dynamic_slice_in_dim(value_head_rows, shared, HEAD_SIZE, 1)
        scores = jnp.dot(query_cols, key_cols.T, preferred_element_type=jnp.float32) * inv_root
        masked = jnp.where(visible, scores, -jnp.inf)
        row_max = jnp.max(masked, axis=1, keepdims=True)
        weights = jnp.where(visible, jnp.exp(masked - row_max), 0.0)
        totals = jnp.sum(weights, axis=1, keepdims=True)
        mixed = jnp.dot(weights.astype(jnp.bfloat16), value_cols, preferred_element_type=jnp.float32)
        return (mixed / totals).astype(jnp.bfloat16)

    heads_out = lax.map(one_head, jnp.arange(QUERY_HEADS, dtype=jnp.int32))
    attention = heads_out.transpose(1, 0, 2).reshape(SEQUENCE_TOKENS, QUERY_HEADS * HEAD_SIZE)
    span = HPD * HEAD_SIZE

    def add_group(running, group_number):
        features = lax.dynamic_slice_in_dim(attention, group_number * span, span, 1)
        weight_rows = lax.dynamic_slice_in_dim(out_weight, group_number * span, span, 0)
        partial_value = jnp.dot(features, weight_rows, preferred_element_type=jnp.float32).astype(jnp.bfloat16)
        return running + partial_value.astype(jnp.float32), None

    running, _ = lax.scan(add_group, jnp.zeros((SEQUENCE_TOKENS, DOUT), jnp.float32), jnp.arange(N_HEADS, dtype=jnp.int32))
    return running.astype(jnp.bfloat16)
```

```python
import functools
import math

import jax
import jax.numpy as jnp
from jax import lax
from jax.experimental import pallas as pl
from jax.experimental.pallas import tpu as pltpu
from jax.sharding import PartitionSpec as P

QUERY_HEADS = 64
KEY_VALUE_HEADS = 8
HEAD_SIZE = 128
MASKED_SCORE = -1e30
COLUMN_STEP = 256
F32 = jnp.float32
BF16 = jnp.bfloat16


def kernel(nb, nh, q_ref, k_ref, v_ref, w_ref, out_ref,
           kbuf, vbuf, wbuf, acc, top, att, ysend, yrecv, zsend, zrecv,
           local_sem, kv_send, kv_recv, relay_send, w_send, w_recv,
           att_send, att_recv, y_send, y_recv, z_send, z_recv):
    nx, nz = nb // 2, nh // 2
    rows = k_ref.shape[0]
    piece = rows // nh
    half = rows // 2
    heads = q_ref.shape[3] // HEAD_SIZE
    depth, wcols = w_ref.shape
    step = wbuf.shape[3]
    ns = wcols // step
    scale = math.log2(math.e) * HEAD_SIZE ** (-0.5)

    b, h = lax.axis_index("blk"), lax.axis_index("heads")
    x, c = b // 2, b % 2
    z, y = h // 2, h % 2
    partner = x * 2 + (1 - c)
    kv_col = pl.multiple_of((h * heads // (QUERY_HEADS // KEY_VALUE_HEADS)) * HEAD_SIZE, HEAD_SIZE)

    def remote(src, dst, ssem, rsem, blk, hd):
        return pltpu.make_async_remote_copy(
            src_ref=src, dst_ref=dst, send_sem=ssem, recv_sem=rsem,
            device_id=(blk, hd), device_id_type=pl.DeviceIdType.MESH)

    k_own = k_ref.at[:, pl.ds(kv_col, HEAD_SIZE)]
    v_own = v_ref.at[:, pl.ds(kv_col, HEAD_SIZE)]
    local_k = pltpu.make_async_copy(k_own, kbuf.at[b], local_sem.at[0])
    local_v = pltpu.make_async_copy(v_own, vbuf.at[b], local_sem.at[1])
    local_k.start()
    local_v.start()

    def w_cols(s):
        return w_ref.at[:, pl.ds(s * step, step)]

    local_w = [pltpu.make_async_copy(w_cols(s), wbuf.at[x, s], local_sem.at[2 + s]) for s in range(ns)]
    for copy in local_w:
        copy.start()

    barrier = pltpu.get_barrier_semaphore()

    def greet(blk, hd):
        pl.semaphore_signal(barrier, inc=1, device_id=(blk, hd), device_id_type=pl.DeviceIdType.MESH)

    for i in range(1, nx):
        greet(lax.rem(x + i, nx) * 2 + c, h)
    greet(b, z * 2 + (1 - y))

    def greet_owner(d, carry):
        @pl.when(d != c * nz + z)
        def _():
            greet(x * 2 + d // nz, (d % nz) * 2 + y)
        return carry

    lax.fori_loop(0, 2 * nz, greet_owner, 0)
    pl.semaphore_wait(barrier, nx - 1 + 1 + 2 * nz - 1)

    def kv_copy(buf, own, n, src_blk, dst_blk, ssem):
        return remote(own, buf.at[src_blk], ssem, kv_recv.at[n, src_blk], dst_blk, h)

    @pl.when(c == 0)
    def _():
        for n, (buf, own) in enumerate(((kbuf, k_own), (vbuf, v_own))):
            kv_copy(buf, own, n, b, partner, kv_send.at[n, nx]).start()

    for j in range(1, nx):
        @pl.when(j > x)
        def _():
            for n, (buf, own) in enumerate(((kbuf, k_own), (vbuf, v_own))):
                kv_copy(buf, own, n, b, j * 2 + c, kv_send.at[n, j]).start()

    for s in range(ns):
        for i in range(1, nx):
            to = lax.rem(x + i, nx)
            remote(w_cols(s), wbuf.at[x, s], w_send.at[i, s], w_recv.at[x, s], to * 2 + c, h).start()

    def group_y(g):
        return (1 - y) if g == 0 else y

    def scores_of(g, hd, j):
        cols = pl.ds(pl.multiple_of(hd * HEAD_SIZE, HEAD_SIZE), HEAD_SIZE)
        q = q_ref[:, group_y(g), :, cols].reshape(half, HEAD_SIZE)
        s = lax.dot_general(q, kbuf[j], (((1,), (1,)), ((), ())), preferred_element_type=F32)
        return s * scale

    def mixed_of(p, j):
        v = jnp.concatenate([vbuf[j], jnp.ones((rows, HEAD_SIZE), BF16)], axis=1)
        return jnp.dot(p.astype(BF16), v, preferred_element_type=F32)

    def own_block(g):
        row = lax.broadcasted_iota(jnp.int32, (half, rows), 0)
        position = (row // piece * 2 + group_y(g)) * piece + row % piece
        visible = position >= lax.broadcasted_iota(jnp.int32, (half, rows), 1)

        def one(hd, carry):
            s = jnp.where(visible, scores_of(g, hd, b), MASKED_SCORE)
            m = jnp.max(s, axis=1, keepdims=True)
            acc[g, hd] = mixed_of(jnp.exp2(s - m), b)
            top[g, hd] = jnp.broadcast_to(m, (half, HEAD_SIZE))
            return carry

        lax.fori_loop(0, heads, one, 0, unroll=2)

    def other_block(g, j):
        def one(hd, carry):
            s = scores_of(g, hd, j)
            old = top[g, hd][:, :1]
            m = jnp.maximum(old, jnp.max(s, axis=1, keepdims=True))
            acc[g, hd] = acc[g, hd] * jnp.exp2(old - m) + mixed_of(jnp.exp2(s - m), j)
            top[g, hd] = jnp.broadcast_to(m, (half, HEAD_SIZE))
            return carry

        lax.fori_loop(0, heads, one, 0, unroll=2)

    mine = pl.ds(pl.multiple_of(c * half, half), half)
    theirs = pl.ds(pl.multiple_of((1 - c) * half, half), half)

    def att_copy(g, where):
        return remote(att.at[g, where], att.at[g, where], att_send.at[g], att_recv.at[g], partner, h)

    def finish(g):
        def one(hd, carry):
            cols = pl.ds(pl.multiple_of(hd * HEAD_SIZE, HEAD_SIZE), HEAD_SIZE)
            a = acc[g, hd]
            att[g, mine, cols] = (a[:, :HEAD_SIZE] / a[:, HEAD_SIZE:]).astype(BF16)
            return carry

        lax.fori_loop(0, heads, one, 0)
        att_copy(g, mine).start()

    def others(g):
        @pl.when(c == 1)
        def _():
            other_block(g, b - 1)

        def one(j, carry):
            other_block(g, j)
            return carry

        lax.fori_loop(0, 2 * x, one, 0)

    local_k.wait()
    local_v.wait()
    own_block(0)
    own_block(1)

    @pl.when(c == 1)
    def _():
        for n, (buf, own) in enumerate(((kbuf, k_own), (vbuf, v_own))):
            kv_copy(buf, own, n, b - 1, partner, kv_send.at[n, nx]).wait_recv()

    for j in range(nx - 1):
        @pl.when(j < x)
        def _():
            for n, (buf, own) in enumerate(((kbuf, k_own), (vbuf, v_own))):
                at = j * 2 + c
                kv_copy(buf, own, n, at, partner, kv_send.at[n, 0]).wait_recv()
                kv_copy(buf, buf.at[at], n, at, partner, relay_send.at[n, j]).start()

    for j in range(nx - 1):
        @pl.when(j < x)
        def _():
            for n, (buf, own) in enumerate(((kbuf, k_own), (vbuf, v_own))):
                kv_copy(buf, own, n, j * 2 + 1 - c, partner, kv_send.at[n, 0]).wait_recv()

    others(0)
    finish(0)

    chunks = [(i, s) for i in range(nx) for s in range(ns)]

    def from_chip(i):
        return x if i == 0 else lax.rem(x + nx - i, nx)

    def y_copy(k):
        return remote(ysend.at[k], yrecv.at[k], y_send.at[k], y_recv.at[k], b, z * 2 + (1 - y))

    def first(k):
        i, s = chunks[k]
        if i == 0:
            local_w[s].wait()
        else:
            remote(w_cols(s), wbuf.at[from_chip(i), s], w_send.at[i, s], w_recv.at[from_chip(i), s], partner, h).wait_recv()
        d = jnp.dot(att[0], wbuf[from_chip(i), s], preferred_element_type=F32)
        ysend[k] = d.astype(BF16)
        y_copy(k).start()

    def z_copy(k, d, src_z, src_c):
        return remote(zsend.at[k, d], zrecv.at[k, src_c * nz + src_z], z_send.at[k, d],
                      z_recv.at[k, src_c * nz + src_z], x * 2 + d // nz, (d % nz) * 2 + y)

    seat = c * nz + z

    def second(k):
        i, s = chunks[k]
        d = jnp.dot(att[1], wbuf[from_chip(i), s], preferred_element_type=F32)
        y_copy(k).wait_recv()
        d = (d + yrecv[k].astype(F32)).astype(BF16)
        zsend[k] = d.reshape(2 * nz, piece, step)

        def push(t, carry):
            to = lax.rem(seat + t, 2 * nz)
            z_copy(k, to, z, c).start()
            return carry

        lax.fori_loop(1, 2 * nz, push, 0)
        zrecv[k, seat] = zsend[k, seat]

    att_copy(0, theirs).wait_recv()
    for k in range(ns):
        first(k)
    others(1)
    finish(1)
    done = 0
    for k in range(ns, len(chunks)):
        first(k)
        if done == 0:
            att_copy(1, theirs).wait_recv()
        while done < k:
            second(done)
            done += 1
    if done == 0:
        att_copy(1, theirs).wait_recv()
    while done < len(chunks):
        second(done)
        done += 1

    for k, (i, s) in enumerate(chunks):
        def landed(t, carry):
            src = lax.rem(seat + t, 2 * nz)
            z_copy(k, src, src % nz, src // nz).wait_recv()
            return carry

        lax.fori_loop(1, 2 * nz, landed, 0)
        for src_c in range(2):
            total = zrecv[k, src_c * nz].astype(F32)
            for src_z in range(1, nz):
                total += zrecv[k, src_c * nz + src_z].astype(F32)
            col = pl.multiple_of((from_chip(i) * 2 + src_c) * wcols + s * step, step)
            out_ref[:, pl.ds(col, step)] = total.astype(BF16)

    @pl.when(c == 0)
    def _():
        for n, (buf, own) in enumerate(((kbuf, k_own), (vbuf, v_own))):
            kv_copy(buf, own, n, b, partner, kv_send.at[n, nx]).wait_send()

    for j in range(1, nx):
        @pl.when(j > x)
        def _():
            for n, (buf, own) in enumerate(((kbuf, k_own), (vbuf, v_own))):
                kv_copy(buf, own, n, b, j * 2 + c, kv_send.at[n, j]).wait_send()

    for j in range(nx - 1):
        @pl.when(j < x)
        def _():
            for n, (buf, own) in enumerate(((kbuf, k_own), (vbuf, v_own))):
                at = j * 2 + c
                kv_copy(buf, buf.at[at], n, at, partner, relay_send.at[n, j]).wait_send()

    for s in range(ns):
        for i in range(1, nx):
            remote(w_cols(s), wbuf.at[x, s], w_send.at[i, s], w_recv.at[x, s], partner, h).wait_send()
    for g in range(2):
        att_copy(g, mine).wait_send()
    for k in range(len(chunks)):
        y_copy(k).wait_send()

        def left(t, carry):
            z_copy(k, lax.rem(seat + t, 2 * nz), z, c).wait_send()
            return carry

        lax.fori_loop(1, 2 * nz, left, 0)


def shards(nb, nh, queries, key_rows, value_head_rows, out_weight):
    rows, qcols = queries.shape
    depth, wcols = out_weight.shape
    heads = qcols // HEAD_SIZE
    nx, nz = nb // 2, nh // 2
    piece, half = rows // nh, rows // 2
    step = math.gcd(wcols, COLUMN_STEP)
    ns = wcols // step
    nk = nx * ns
    q = queries.reshape(nz, 2, piece, qcols)
    dma = pltpu.SemaphoreType.DMA
    vmem = pl.BlockSpec(memory_space=pltpu.VMEM)
    hbm = pl.BlockSpec(memory_space=pl.ANY)
    return pl.pallas_call(
        functools.partial(kernel, nb, nh),
        out_shape=jax.ShapeDtypeStruct((piece, wcols * nb), BF16),
        in_specs=[vmem, hbm, hbm, hbm],
        out_specs=vmem,
        scratch_shapes=[
            pltpu.VMEM((nb, rows, HEAD_SIZE), BF16),
            pltpu.VMEM((nb, rows, HEAD_SIZE), BF16),
            pltpu.VMEM((nx, ns, depth, step), BF16),
            pltpu.VMEM((2, heads, half, 2 * HEAD_SIZE), F32),
            pltpu.VMEM((2, heads, half, HEAD_SIZE), F32),
            pltpu.VMEM((2, 2 * half, qcols), BF16),
            pltpu.VMEM((nk, 2 * half, step), BF16),
            pltpu.VMEM((nk, 2 * half, step), BF16),
            pltpu.VMEM((nk, 2 * nz, piece, step), BF16),
            pltpu.VMEM((nk, 2 * nz, piece, step), BF16),
            dma((2 + ns,)),
            dma((2, nx + 1)),
            dma((2, nb)),
            dma((2, nx)),
            dma((nx, ns)),
            dma((nx, ns)),
            dma((2,)),
            dma((2,)),
            dma((nk,)),
            dma((nk,)),
            dma((nk, 2 * nz)),
            dma((nk, 2 * nz)),
        ],
        compiler_params=pltpu.CompilerParams(
            collective_id=0, has_side_effects=True, vmem_limit_bytes=50 * 2**20),
    )(q, key_rows, value_head_rows, out_weight)


def solution(mesh):
    in_specs = (P("blk", "heads"), P("blk", None), P("blk", None), P("heads", "blk"))
    out_specs = P(("blk", "heads"), None)
    body = functools.partial(shards, mesh.shape["blk"], mesh.shape["heads"])
    return jax.shard_map(body, mesh=mesh, in_specs=in_specs, out_specs=out_specs, check_vma=False)
```

```python
import functools
import math

import jax
import jax.numpy as jnp
from jax import lax
from jax.experimental import pallas as pl
from jax.experimental.pallas import tpu as pltpu
from jax.sharding import PartitionSpec as P

QUERY_HEADS = 64
KEY_VALUE_HEADS = 8
HEAD_SIZE = 128
MASKED_SCORE = -1e30
COLUMN_STEP = 256
TOTAL_ROWS = 16
F32 = jnp.float32
BF16 = jnp.bfloat16


def kernel(nb, nh, q_hbm, k_ref, v_ref, w_ref, out_ref,
           q_ref, kbuf, vbuf, vturn, wbuf, acc, top, att, ysend, yrecv, zsend, zrecv,
           local_sem, kv_send, kv_recv, relay_send, w_send, w_recv,
           att_send, att_recv, y_send, y_recv, z_send, z_recv):
    nx, nz = nb // 2, nh // 2
    rows = k_ref.shape[0]
    piece = rows // nh
    half = rows // 2
    heads = q_ref.shape[3] // HEAD_SIZE
    depth, wcols = w_ref.shape
    step = wbuf.shape[3]
    ns = wcols // step
    scale = math.log2(math.e) * HEAD_SIZE ** (-0.5)

    b, h = lax.axis_index("blk"), lax.axis_index("heads")
    x, c = b // 2, b % 2
    z, y = h // 2, h % 2
    partner = x * 2 + (1 - c)
    kv_col = pl.multiple_of((h * heads // (QUERY_HEADS // KEY_VALUE_HEADS)) * HEAD_SIZE, HEAD_SIZE)

    def remote(src, dst, ssem, rsem, blk, hd):
        return pltpu.make_async_remote_copy(
            src_ref=src, dst_ref=dst, send_sem=ssem, recv_sem=rsem,
            device_id=(blk, hd), device_id_type=pl.DeviceIdType.MESH)

    k_own = k_ref.at[:, pl.ds(kv_col, HEAD_SIZE)]
    v_own = v_ref.at[:, pl.ds(kv_col, HEAD_SIZE)]
    local_k = pltpu.make_async_copy(k_own, kbuf.at[b], local_sem.at[0])
    local_v = pltpu.make_async_copy(v_own, vbuf.at[b], local_sem.at[1])
    local_q = pltpu.make_async_copy(q_hbm, q_ref, local_sem.at[2 + ns])
    local_k.start()
    local_v.start()
    local_q.start()

    def w_cols(s):
        return w_ref.at[:, pl.ds(s * step, step)]

    local_w = [pltpu.make_async_copy(w_cols(s), wbuf.at[x, s], local_sem.at[2 + s]) for s in range(ns)]
    for copy in local_w:
        copy.start()

    barrier = pltpu.get_barrier_semaphore()

    def greet(blk, hd):
        pl.semaphore_signal(barrier, inc=1, device_id=(blk, hd), device_id_type=pl.DeviceIdType.MESH)

    for i in range(1, nx):
        greet(lax.rem(x + i, nx) * 2 + c, h)
    greet(b, z * 2 + (1 - y))

    def greet_owner(d, carry):
        @pl.when(d != c * nz + z)
        def _():
            greet(x * 2 + d // nz, (d % nz) * 2 + y)
        return carry

    lax.fori_loop(0, 2 * nz, greet_owner, 0)
    pl.semaphore_wait(barrier, nx - 1 + 1 + 2 * nz - 1)

    def kv_copy(buf, own, n, src_blk, dst_blk, ssem):
        return remote(own, buf.at[src_blk], ssem, kv_recv.at[n, src_blk], dst_blk, h)

    @pl.when(c == 0)
    def _():
        for n, (buf, own) in enumerate(((kbuf, k_own), (vbuf, v_own))):
            kv_copy(buf, own, n, b, partner, kv_send.at[n, nx]).start()

    for j in range(1, nx):
        @pl.when(j > x)
        def _():
            for n, (buf, own) in enumerate(((kbuf, k_own), (vbuf, v_own))):
                kv_copy(buf, own, n, b, j * 2 + c, kv_send.at[n, j]).start()

    for s in range(ns):
        for i in range(1, nx):
            to = lax.rem(x + i, nx)
            remote(w_cols(s), wbuf.at[x, s], w_send.at[i, s], w_recv.at[x, s], to * 2 + c, h).start()

    def group_y(g):
        return (1 - y) if g == 0 else y

    def scores_of(g, hd, j):
        cols = pl.ds(pl.multiple_of(hd * HEAD_SIZE, HEAD_SIZE), HEAD_SIZE)
        q = q_ref[:, group_y(g), :, cols].reshape(half, HEAD_SIZE)
        s = lax.dot_general(kbuf[j], q, (((1,), (1,)), ((), ())), preferred_element_type=F32)
        return s * scale

    def turn(j):
        vturn[j, :HEAD_SIZE] = vbuf[j].T
        vturn[j, HEAD_SIZE:] = jnp.ones((TOTAL_ROWS, rows), BF16)

    def mixed_of(p, j):
        return jnp.dot(vturn[j], p.astype(BF16), preferred_element_type=F32)

    def own_block(g):
        row = lax.broadcasted_iota(jnp.int32, (rows, half), 1)
        position = (row // piece * 2 + group_y(g)) * piece + row % piece
        visible = position >= lax.broadcasted_iota(jnp.int32, (rows, half), 0)

        def one(hd, carry):
            s = jnp.where(visible, scores_of(g, hd, b), MASKED_SCORE)
            m = jnp.max(s, axis=0, keepdims=True)
            acc[g, hd] = mixed_of(jnp.exp2(s - m), b)
            top[g, hd] = jnp.broadcast_to(m, (8, half))
            return carry

        lax.fori_loop(0, heads, one, 0, unroll=2)

    def other_block(g, j):
        def one(hd, carry):
            s = scores_of(g, hd, j)
            old = top[g, hd][:1]
            m = jnp.maximum(old, jnp.max(s, axis=0, keepdims=True))
            acc[g, hd] = acc[g, hd] * jnp.exp2(old - m) + mixed_of(jnp.exp2(s - m), j)
            top[g, hd] = jnp.broadcast_to(m, (8, half))
            return carry

        lax.fori_loop(0, heads, one, 0, unroll=2)

    mine = pl.ds(pl.multiple_of(c * half, half), half)
    theirs = pl.ds(pl.multiple_of((1 - c) * half, half), half)

    def att_copy(g, where):
        return remote(att.at[g, where], att.at[g, where], att_send.at[g], att_recv.at[g], partner, h)

    def finish(g):
        def one(hd, carry):
            cols = pl.ds(pl.multiple_of(hd * HEAD_SIZE, HEAD_SIZE), HEAD_SIZE)
            a = acc[g, hd]
            att[g, mine, cols] = (a[:HEAD_SIZE] / a[HEAD_SIZE:HEAD_SIZE + 1]).T.astype(BF16)
            return carry

        lax.fori_loop(0, heads, one, 0)
        att_copy(g, mine).start()

    def others(g):
        @pl.when(c == 1)
        def _():
            other_block(g, b - 1)

        def one(j, carry):
            other_block(g, j)
            return carry

        lax.fori_loop(0, 2 * x, one, 0)

    local_k.wait()
    local_v.wait()
    turn(b)
    local_q.wait()
    own_block(0)
    own_block(1)

    @pl.when(c == 1)
    def _():
        for n, (buf, own) in enumerate(((kbuf, k_own), (vbuf, v_own))):
            kv_copy(buf, own, n, b - 1, partner, kv_send.at[n, nx]).wait_recv()
        turn(b - 1)

    for j in range(nx - 1):
        @pl.when(j < x)
        def _():
            for n, (buf, own) in enumerate(((kbuf, k_own), (vbuf, v_own))):
                at = j * 2 + c
                kv_copy(buf, own, n, at, partner, kv_send.at[n, 0]).wait_recv()
                kv_copy(buf, buf.at[at], n, at, partner, relay_send.at[n, j]).start()

    for j in range(nx - 1):
        @pl.when(j < x)
        def _():
            for n, (buf, own) in enumerate(((kbuf, k_own), (vbuf, v_own))):
                kv_copy(buf, own, n, j * 2 + 1 - c, partner, kv_send.at[n, 0]).wait_recv()
            turn(j * 2)
            turn(j * 2 + 1)

    others(0)
    finish(0)

    chunks = [(i, s) for i in range(nx) for s in range(ns)]

    def from_chip(i):
        return x if i == 0 else lax.rem(x + nx - i, nx)

    def y_copy(k):
        return remote(ysend.at[k], yrecv.at[k], y_send.at[k], y_recv.at[k], b, z * 2 + (1 - y))

    def first(k):
        i, s = chunks[k]
        if i == 0:
            local_w[s].wait()
        else:
            remote(w_cols(s), wbuf.at[from_chip(i), s], w_send.at[i, s], w_recv.at[from_chip(i), s], partner, h).wait_recv()
        d = jnp.dot(att[0], wbuf[from_chip(i), s], preferred_element_type=F32)
        ysend[k] = d.astype(BF16)
        y_copy(k).start()

    def z_copy(k, d, src_z, src_c):
        return remote(zsend.at[k, d], zrecv.at[k, src_c * nz + src_z], z_send.at[k, d],
                      z_recv.at[k, src_c * nz + src_z], x * 2 + d // nz, (d % nz) * 2 + y)

    seat = c * nz + z

    def second(k):
        i, s = chunks[k]
        d = jnp.dot(att[1], wbuf[from_chip(i), s], preferred_element_type=F32)
        y_copy(k).wait_recv()
        d = (d + yrecv[k].astype(F32)).astype(BF16)
        zsend[k] = d.reshape(2 * nz, piece, step)

        def push(t, carry):
            to = lax.rem(seat + t, 2 * nz)
            z_copy(k, to, z, c).start()
            return carry

        lax.fori_loop(1, 2 * nz, push, 0)
        zrecv[k, seat] = zsend[k, seat]

    att_copy(0, theirs).wait_recv()
    for k in range(ns):
        first(k)
    others(1)
    finish(1)
    done = 0
    for k in range(ns, len(chunks)):
        first(k)
        if done == 0:
            att_copy(1, theirs).wait_recv()
        while done < k:
            second(done)
            done += 1
    if done == 0:
        att_copy(1, theirs).wait_recv()
    while done < len(chunks):
        second(done)
        done += 1

    for k, (i, s) in enumerate(chunks):
        def landed(t, carry):
            src = lax.rem(seat + t, 2 * nz)
            z_copy(k, src, src % nz, src // nz).wait_recv()
            return carry

        lax.fori_loop(1, 2 * nz, landed, 0)
        for src_c in range(2):
            total = zrecv[k, src_c * nz].astype(F32)
            for src_z in range(1, nz):
                total += zrecv[k, src_c * nz + src_z].astype(F32)
            col = pl.multiple_of((from_chip(i) * 2 + src_c) * wcols + s * step, step)
            out_ref[:, pl.ds(col, step)] = total.astype(BF16)

    @pl.when(c == 0)
    def _():
        for n, (buf, own) in enumerate(((kbuf, k_own), (vbuf, v_own))):
            kv_copy(buf, own, n, b, partner, kv_send.at[n, nx]).wait_send()

    for j in range(1, nx):
        @pl.when(j > x)
        def _():
            for n, (buf, own) in enumerate(((kbuf, k_own), (vbuf, v_own))):
                kv_copy(buf, own, n, b, j * 2 + c, kv_send.at[n, j]).wait_send()

    for j in range(nx - 1):
        @pl.when(j < x)
        def _():
            for n, (buf, own) in enumerate(((kbuf, k_own), (vbuf, v_own))):
                at = j * 2 + c
                kv_copy(buf, buf.at[at], n, at, partner, relay_send.at[n, j]).wait_send()

    for s in range(ns):
        for i in range(1, nx):
            remote(w_cols(s), wbuf.at[x, s], w_send.at[i, s], w_recv.at[x, s], partner, h).wait_send()
    for g in range(2):
        att_copy(g, mine).wait_send()
    for k in range(len(chunks)):
        y_copy(k).wait_send()

        def left(t, carry):
            z_copy(k, lax.rem(seat + t, 2 * nz), z, c).wait_send()
            return carry

        lax.fori_loop(1, 2 * nz, left, 0)


def shards(nb, nh, queries, key_rows, value_head_rows, out_weight):
    rows, qcols = queries.shape
    depth, wcols = out_weight.shape
    heads = qcols // HEAD_SIZE
    nx, nz = nb // 2, nh // 2
    piece, half = rows // nh, rows // 2
    step = math.gcd(wcols, COLUMN_STEP)
    ns = wcols // step
    nk = nx * ns
    q = queries.reshape(nz, 2, piece, qcols)
    dma = pltpu.SemaphoreType.DMA
    vmem = pl.BlockSpec(memory_space=pltpu.VMEM)
    hbm = pl.BlockSpec(memory_space=pl.ANY)
    return pl.pallas_call(
        functools.partial(kernel, nb, nh),
        out_shape=jax.ShapeDtypeStruct((piece, wcols * nb), BF16),
        in_specs=[hbm, hbm, hbm, hbm],
        out_specs=vmem,
        scratch_shapes=[
            pltpu.VMEM((nz, 2, piece, qcols), BF16),
            pltpu.VMEM((nb, rows, HEAD_SIZE), BF16),
            pltpu.VMEM((nb, rows, HEAD_SIZE), BF16),
            pltpu.VMEM((nb, HEAD_SIZE + TOTAL_ROWS, rows), BF16),
            pltpu.VMEM((nx, ns, depth, step), BF16),
            pltpu.VMEM((2, heads, HEAD_SIZE + TOTAL_ROWS, half), F32),
            pltpu.VMEM((2, heads, 8, half), F32),
            pltpu.VMEM((2, 2 * half, qcols), BF16),
            pltpu.VMEM((nk, 2 * half, step), BF16),
            pltpu.VMEM((nk, 2 * half, step), BF16),
            pltpu.VMEM((nk, 2 * nz, piece, step), BF16),
            pltpu.VMEM((nk, 2 * nz, piece, step), BF16),
            dma((3 + ns,)),
            dma((2, nx + 1)),
            dma((2, nb)),
            dma((2, nx)),
            dma((nx, ns)),
            dma((nx, ns)),
            dma((2,)),
            dma((2,)),
            dma((nk,)),
            dma((nk,)),
            dma((nk, 2 * nz)),
            dma((nk, 2 * nz)),
        ],
        compiler_params=pltpu.CompilerParams(
            collective_id=0, has_side_effects=True, vmem_limit_bytes=66_000_000),
    )(q, key_rows, value_head_rows, out_weight)


def solution(mesh):
    in_specs = (P("blk", "heads"), P("blk", None), P("blk", None), P("heads", "blk"))
    out_specs = P(("blk", "heads"), None)
    body = functools.partial(shards, mesh.shape["blk"], mesh.shape["heads"])
    return jax.shard_map(body, mesh=mesh, in_specs=in_specs, out_specs=out_specs, check_vma=False)
```

```python
import functools
import math

import jax
import jax.numpy as jnp
from jax import lax
from jax.experimental import pallas as pl
from jax.experimental.pallas import tpu as pltpu
from jax.sharding import PartitionSpec as P

QUERY_HEADS = 64
KEY_VALUE_HEADS = 8
HEAD_SIZE = 128
MASKED_SCORE = -1e30
COLUMN_STEP = 256
TOTAL_ROWS = 16
KEY_TILE = 256
F32 = jnp.float32
BF16 = jnp.bfloat16


def kernel(nb, nh, q_hbm, k_ref, v_ref, w_ref, out_ref,
           q_ref, kbuf, vbuf, vturn, wbuf, sbuf, mbuf, acc, top, att, ysend, yrecv, zsend, zrecv,
           local_sem, kv_send, kv_recv, relay_send, w_send, w_recv,
           att_send, att_recv, y_send, y_recv, z_send, z_recv):
    nx, nz = nb // 2, nh // 2
    rows = k_ref.shape[0]
    piece = rows // nh
    half = rows // 2
    heads = q_ref.shape[3] // HEAD_SIZE
    depth, wcols = w_ref.shape
    step = wbuf.shape[3]
    ns = wcols // step
    scale = math.log2(math.e) * HEAD_SIZE ** (-0.5)

    b, h = lax.axis_index("blk"), lax.axis_index("heads")
    x, c = b // 2, b % 2
    z, y = h // 2, h % 2
    partner = x * 2 + (1 - c)
    kv_col = pl.multiple_of((h * heads // (QUERY_HEADS // KEY_VALUE_HEADS)) * HEAD_SIZE, HEAD_SIZE)

    def remote(src, dst, ssem, rsem, blk, hd):
        return pltpu.make_async_remote_copy(
            src_ref=src, dst_ref=dst, send_sem=ssem, recv_sem=rsem,
            device_id=(blk, hd), device_id_type=pl.DeviceIdType.MESH)

    k_own = k_ref.at[:, pl.ds(kv_col, HEAD_SIZE)]
    v_own = v_ref.at[:, pl.ds(kv_col, HEAD_SIZE)]
    local_k = pltpu.make_async_copy(k_own, kbuf.at[b], local_sem.at[0])
    local_v = pltpu.make_async_copy(v_own, vbuf.at[b], local_sem.at[1])
    local_q = pltpu.make_async_copy(q_hbm, q_ref, local_sem.at[2 + ns])
    local_k.start()
    local_v.start()
    local_q.start()

    def w_cols(s):
        return w_ref.at[:, pl.ds(s * step, step)]

    local_w = [pltpu.make_async_copy(w_cols(s), wbuf.at[x, s], local_sem.at[2 + s]) for s in range(ns)]
    for copy in local_w:
        copy.start()

    barrier = pltpu.get_barrier_semaphore()

    def greet(blk, hd):
        pl.semaphore_signal(barrier, inc=1, device_id=(blk, hd), device_id_type=pl.DeviceIdType.MESH)

    for i in range(1, nx):
        greet(lax.rem(x + i, nx) * 2 + c, h)
    greet(b, z * 2 + (1 - y))

    def greet_owner(d, carry):
        @pl.when(d != c * nz + z)
        def _():
            greet(x * 2 + d // nz, (d % nz) * 2 + y)
        return carry

    lax.fori_loop(0, 2 * nz, greet_owner, 0)
    pl.semaphore_wait(barrier, nx - 1 + 1 + 2 * nz - 1)

    def kv_copy(buf, own, n, src_blk, dst_blk, ssem):
        return remote(own, buf.at[src_blk], ssem, kv_recv.at[n, src_blk], dst_blk, h)

    @pl.when(c == 0)
    def _():
        for n, (buf, own) in enumerate(((kbuf, k_own), (vbuf, v_own))):
            kv_copy(buf, own, n, b, partner, kv_send.at[n, nx]).start()

    for j in range(1, nx):
        @pl.when(j > x)
        def _():
            for n, (buf, own) in enumerate(((kbuf, k_own), (vbuf, v_own))):
                kv_copy(buf, own, n, b, j * 2 + c, kv_send.at[n, j]).start()

    for s in range(ns):
        for i in range(1, nx):
            to = lax.rem(x + i, nx)
            remote(w_cols(s), wbuf.at[x, s], w_send.at[i, s], w_recv.at[x, s], to * 2 + c, h).start()

    def group_y(g):
        return (1 - y) if g == 0 else y

    def turn(j):
        vturn[j, :HEAD_SIZE] = vbuf[j].T
        vturn[j, HEAD_SIZE:] = jnp.ones((TOTAL_ROWS, rows), BF16)

    tile = sbuf.shape[2]
    tiles = rows // tile

    def score_tile(g, hd, j, t, own):
        cols = pl.ds(pl.multiple_of(hd * HEAD_SIZE, HEAD_SIZE), HEAD_SIZE)
        q = q_ref[:, group_y(g), :, cols].reshape(half, HEAD_SIZE)
        k = kbuf[j, t * tile:(t + 1) * tile]
        s = lax.dot_general(k, q, (((1,), (1,)), ((), ())), preferred_element_type=F32) * scale
        if own:
            row = lax.broadcasted_iota(jnp.int32, (tile, half), 1)
            position = (row // piece * 2 + group_y(g)) * piece + row % piece
            visible = position >= lax.broadcasted_iota(jnp.int32, (tile, half), 0) + t * tile
            s = jnp.where(visible, s, MASKED_SCORE)
        return s

    def block(g, j, own):
        def put(hd, slot, t, m):
            s = score_tile(g, hd, j, t, own)
            sbuf[slot, t] = s
            n = jnp.max(s, axis=0, keepdims=True)
            return n if m is None else jnp.maximum(m, n)

        def step(hd, following, slot):
            m = mbuf[slot][:1]
            if not own:
                old = top[g, hd][:1]
                m = jnp.maximum(old, m)
            mixed, ahead = None, None
            for t in range(tiles):
                ahead = put(following, 1 - slot, t, ahead)
                p = jnp.exp2(sbuf[slot, t] - m).astype(BF16)
                d = jnp.dot(vturn[j, :, t * tile:(t + 1) * tile], p, preferred_element_type=F32)
                mixed = d if mixed is None else mixed + d
            mbuf[1 - slot] = jnp.broadcast_to(ahead, (8, half))
            if not own:
                mixed += acc[g, hd] * jnp.exp2(old - m)
            acc[g, hd] = mixed
            top[g, hd] = jnp.broadcast_to(m, (8, half))

        ahead = None
        for t in range(tiles):
            ahead = put(0, 0, t, ahead)
        mbuf[0] = jnp.broadcast_to(ahead, (8, half))

        def pair(i, carry):
            step(2 * i, 2 * i + 1, 0)
            step(2 * i + 1, jnp.minimum(2 * i + 2, heads - 1), 1)
            return carry

        lax.fori_loop(0, heads // 2, pair, 0)

    mine = pl.ds(pl.multiple_of(c * half, half), half)
    theirs = pl.ds(pl.multiple_of((1 - c) * half, half), half)

    def att_copy(g, where):
        return remote(att.at[g, where], att.at[g, where], att_send.at[g], att_recv.at[g], partner, h)

    def finish(g):
        def one(hd, carry):
            cols = pl.ds(pl.multiple_of(hd * HEAD_SIZE, HEAD_SIZE), HEAD_SIZE)
            a = acc[g, hd]
            att[g, mine, cols] = (a[:HEAD_SIZE] / a[HEAD_SIZE:HEAD_SIZE + 1]).T.astype(BF16)
            return carry

        lax.fori_loop(0, heads, one, 0)
        att_copy(g, mine).start()

    def others(g):
        @pl.when(c == 1)
        def _():
            block(g, b - 1, False)

        def one(j, carry):
            block(g, j, False)
            return carry

        lax.fori_loop(0, 2 * x, one, 0)

    local_k.wait()
    local_v.wait()
    turn(b)
    local_q.wait()
    block(0, b, True)
    block(1, b, True)

    @pl.when(c == 1)
    def _():
        for n, (buf, own) in enumerate(((kbuf, k_own), (vbuf, v_own))):
            kv_copy(buf, own, n, b - 1, partner, kv_send.at[n, nx]).wait_recv()
        turn(b - 1)

    for j in range(nx - 1):
        @pl.when(j < x)
        def _():
            for n, (buf, own) in enumerate(((kbuf, k_own), (vbuf, v_own))):
                at = j * 2 + c
                kv_copy(buf, own, n, at, partner, kv_send.at[n, 0]).wait_recv()
                kv_copy(buf, buf.at[at], n, at, partner, relay_send.at[n, j]).start()

    for j in range(nx - 1):
        @pl.when(j < x)
        def _():
            for n, (buf, own) in enumerate(((kbuf, k_own), (vbuf, v_own))):
                kv_copy(buf, own, n, j * 2 + 1 - c, partner, kv_send.at[n, 0]).wait_recv()
            turn(j * 2)
            turn(j * 2 + 1)

    others(0)
    finish(0)

    chunks = [(i, s) for i in range(nx) for s in range(ns)]

    def from_chip(i):
        return x if i == 0 else lax.rem(x + nx - i, nx)

    def y_copy(k):
        return remote(ysend.at[k], yrecv.at[k], y_send.at[k], y_recv.at[k], b, z * 2 + (1 - y))

    def first(k):
        i, s = chunks[k]
        if i == 0:
            local_w[s].wait()
        else:
            remote(w_cols(s), wbuf.at[from_chip(i), s], w_send.at[i, s], w_recv.at[from_chip(i), s], partner, h).wait_recv()
        d = jnp.dot(att[0], wbuf[from_chip(i), s], preferred_element_type=F32)
        ysend[k] = d.astype(BF16)
        y_copy(k).start()

    def z_copy(k, d, src_z, src_c):
        return remote(zsend.at[k, d], zrecv.at[k, src_c * nz + src_z], z_send.at[k, d],
                      z_recv.at[k, src_c * nz + src_z], x * 2 + d // nz, (d % nz) * 2 + y)

    seat = c * nz + z

    def second(k):
        i, s = chunks[k]
        d = jnp.dot(att[1], wbuf[from_chip(i), s], preferred_element_type=F32)
        y_copy(k).wait_recv()
        d = (d + yrecv[k].astype(F32)).astype(BF16)
        zsend[k] = d.reshape(2 * nz, piece, step)

        def push(t, carry):
            to = lax.rem(seat + t, 2 * nz)
            z_copy(k, to, z, c).start()
            return carry

        lax.fori_loop(1, 2 * nz, push, 0)
        zrecv[k, seat] = zsend[k, seat]

    att_copy(0, theirs).wait_recv()
    for k in range(ns):
        first(k)
    others(1)
    finish(1)
    done = 0
    for k in range(ns, len(chunks)):
        first(k)
        if done == 0:
            att_copy(1, theirs).wait_recv()
        while done < k:
            second(done)
            done += 1
    if done == 0:
        att_copy(1, theirs).wait_recv()
    while done < len(chunks):
        second(done)
        done += 1

    for k, (i, s) in enumerate(chunks):
        def landed(t, carry):
            src = lax.rem(seat + t, 2 * nz)
            z_copy(k, src, src % nz, src // nz).wait_recv()
            return carry

        lax.fori_loop(1, 2 * nz, landed, 0)
        for src_c in range(2):
            total = zrecv[k, src_c * nz].astype(F32)
            for src_z in range(1, nz):
                total += zrecv[k, src_c * nz + src_z].astype(F32)
            col = pl.multiple_of((from_chip(i) * 2 + src_c) * wcols + s * step, step)
            out_ref[:, pl.ds(col, step)] = total.astype(BF16)

    @pl.when(c == 0)
    def _():
        for n, (buf, own) in enumerate(((kbuf, k_own), (vbuf, v_own))):
            kv_copy(buf, own, n, b, partner, kv_send.at[n, nx]).wait_send()

    for j in range(1, nx):
        @pl.when(j > x)
        def _():
            for n, (buf, own) in enumerate(((kbuf, k_own), (vbuf, v_own))):
                kv_copy(buf, own, n, b, j * 2 + c, kv_send.at[n, j]).wait_send()

    for j in range(nx - 1):
        @pl.when(j < x)
        def _():
            for n, (buf, own) in enumerate(((kbuf, k_own), (vbuf, v_own))):
                at = j * 2 + c
                kv_copy(buf, buf.at[at], n, at, partner, relay_send.at[n, j]).wait_send()

    for s in range(ns):
        for i in range(1, nx):
            remote(w_cols(s), wbuf.at[x, s], w_send.at[i, s], w_recv.at[x, s], partner, h).wait_send()
    for g in range(2):
        att_copy(g, mine).wait_send()
    for k in range(len(chunks)):
        y_copy(k).wait_send()

        def left(t, carry):
            z_copy(k, lax.rem(seat + t, 2 * nz), z, c).wait_send()
            return carry

        lax.fori_loop(1, 2 * nz, left, 0)


def shards(nb, nh, queries, key_rows, value_head_rows, out_weight):
    rows, qcols = queries.shape
    depth, wcols = out_weight.shape
    heads = qcols // HEAD_SIZE
    nx, nz = nb // 2, nh // 2
    piece, half = rows // nh, rows // 2
    step = math.gcd(wcols, COLUMN_STEP)
    ns = wcols // step
    nk = nx * ns
    tile = math.gcd(rows, KEY_TILE)
    q = queries.reshape(nz, 2, piece, qcols)
    dma = pltpu.SemaphoreType.DMA
    vmem = pl.BlockSpec(memory_space=pltpu.VMEM)
    hbm = pl.BlockSpec(memory_space=pl.ANY)
    return pl.pallas_call(
        functools.partial(kernel, nb, nh),
        out_shape=jax.ShapeDtypeStruct((piece, wcols * nb), BF16),
        in_specs=[hbm, hbm, hbm, hbm],
        out_specs=vmem,
        scratch_shapes=[
            pltpu.VMEM((nz, 2, piece, qcols), BF16),
            pltpu.VMEM((nb, rows, HEAD_SIZE), BF16),
            pltpu.VMEM((nb, rows, HEAD_SIZE), BF16),
            pltpu.VMEM((nb, HEAD_SIZE + TOTAL_ROWS, rows), BF16),
            pltpu.VMEM((nx, ns, depth, step), BF16),
            pltpu.VMEM((2, rows // tile, tile, half), F32),
            pltpu.VMEM((2, 8, half), F32),
            pltpu.VMEM((2, heads, HEAD_SIZE + TOTAL_ROWS, half), F32),
            pltpu.VMEM((2, heads, 8, half), F32),
            pltpu.VMEM((2, 2 * half, qcols), BF16),
            pltpu.VMEM((nk, 2 * half, step), BF16),
            pltpu.VMEM((nk, 2 * half, step), BF16),
            pltpu.VMEM((nk, 2 * nz, piece, step), BF16),
            pltpu.VMEM((nk, 2 * nz, piece, step), BF16),
            dma((3 + ns,)),
            dma((2, nx + 1)),
            dma((2, nb)),
            dma((2, nx)),
            dma((nx, ns)),
            dma((nx, ns)),
            dma((2,)),
            dma((2,)),
            dma((nk,)),
            dma((nk,)),
            dma((nk, 2 * nz)),
            dma((nk, 2 * nz)),
        ],
        compiler_params=pltpu.CompilerParams(
            collective_id=0, has_side_effects=True, vmem_limit_bytes=66_000_000),
    )(q, key_rows, value_head_rows, out_weight)


def solution(mesh):
    in_specs = (P("blk", "heads"), P("blk", None), P("blk", None), P("heads", "blk"))
    out_specs = P(("blk", "heads"), None)
    body = functools.partial(shards, mesh.shape["blk"], mesh.shape["heads"])
    return jax.shard_map(body, mesh=mesh, in_specs=in_specs, out_specs=out_specs, check_vma=False)
```
